512 devices in a mesh: seq: 64 (over x, z), chan: 8 (over y, core).
Axes of the slice: x: 4, y: 4, z: 16, core: 2. Of those that a mesh axis runs over, the one named last changes fastest.
Arguments:
- key_gate: bfloat16 [16384, 8192], P('seq', 'chan'), may hold values from -6 to 6
- values: bfloat16 [16384, 8192], P('seq', 'chan'), may hold values from -6 to 6
- query_gate: bfloat16 [16384, 8192], P('seq', 'chan'), may hold values from -6 to 6
- grad_output: bfloat16 [16384, 8192], P(('seq', 'chan')), may hold values from -6 to 6
- short_taps: bfloat16 [7, 8192], P(None, 'chan'), may hold values from -2 to 2
- long_taps: bfloat16 [128, 8192], P(None, 'chan'), may hold values from -0.5 to 0.5
Outputs:
- grad_query: bfloat16 [16384, 8192], P('seq', 'chan')
- grad_key: bfloat16 [16384, 8192], P('seq', 'chan')
- grad_value: bfloat16 [16384, 8192], P('seq', 'chan')
- grad_long: float32 [128, 8192], P('seq', 'chan')
- grad_short: float32 [7, 8192], P(None, 'chan')
The draws below stay inside these ranges and needn't reach their ends.
All inputs are finite; a program needn't handle non-finite values.
Results may differ from the reference program's by a relative error of at most 0.0059.
Values may be sent and summed in bfloat16 or wider, within the bound.
A program may use at most 64 MiB of HBM per device.

```python
import math
import jax
import jax.numpy as jnp
from jax import lax

D = 8192
MR_TAPS = 128
SE_TAPS = 7
TOKENS = 16384


def steps_of(key, extent, cuts, low, largest):
    def one(position, parts):
        steps = jax.random.uniform(jax.random.fold_in(jax.random.fold_in(key, 6), position), (parts,), jnp.float32, low / len(cuts), largest / len(cuts))
        return jnp.repeat(jnp.exp(steps), extent[position] // parts).reshape((-1,) + (1,) * (len(extent) - position - 1))

    level = one(*cuts[0])
    for cut in cuts[1:]:
        level = level * one(*cut)
    return level


def normal_values(rng, dims, spread, reach, shards=(), kind=jnp.bfloat16):
    entries = jax.random.normal(rng, dims, jnp.float32) * spread
    if len(shards) > 0:
        entries = steps_of(rng, dims, shards, -0.22, 0.18) * entries
    return jnp.clip(entries, min=-reach, max=reach).astype(kind)


def setup_inputs(seed: int = 0) -> dict:
    key_of = jax.random.split(jax.random.key(seed), 7)
    return {
        "key_gate": normal_values(key_of[0], (TOKENS, D), 1.0, 6.0, ((0, 64), (1, 8))),
        "values": normal_values(key_of[1], (TOKENS, D), 1.0, 6.0, ((0, 64), (1, 8))),
        "query_gate": normal_values(key_of[2], (TOKENS, D), 1.0, 6.0, ((0, 64), (1, 8))),
        "grad_output": normal_values(key_of[3], (TOKENS, D), 1.0, 6.0, ((0, 512),)),
        "short_taps": normal_values(key_of[4], (SE_TAPS, D), SE_TAPS ** -0.5, 2.0, ((1, 8),)),
        "long_taps": normal_values(key_of[5], (MR_TAPS, D), MR_TAPS ** -0.5, 0.5, ((1, 8),)),
    }


def causal_short(source, taps):
    length = source.shape[0]
    width = taps.shape[0]
    padded = jnp.pad(source.astype(jnp.float32), ((width - 1, 0), (0, 0)))
    total = jnp.zeros(source.shape, jnp.float32)
    for offset in range(width):
        start = width - 1 - offset
        total = total + taps[offset].astype(jnp.float32)[None, :] * padded[start:start + length]
    return total


def anti_short(source, taps):
    length = source.shape[0]
    width = taps.shape[0]
    padded = jnp.pad(source.astype(jnp.float32), ((0, width - 1), (0, 0)))
    total = jnp.zeros(source.shape, jnp.float32)
    for offset in range(width):
        total = total + taps[offset].astype(jnp.float32)[None, :] * padded[offset:offset + length]
    return total


def filter_short(grad, source, width):
    length = source.shape[0]
    padded = jnp.pad(source.astype(jnp.float32), ((width - 1, 0), (0, 0)))
    gradf = grad.astype(jnp.float32)
    terms = []
    for offset in range(width):
        start = width - 1 - offset
        terms.append(jnp.sum(gradf * padded[start:start + length], axis=0))
    return jnp.stack(terms, 0)


def toeplitz_parts(taps):
    width = taps.shape[0]
    rowsp = jnp.arange(width, dtype=jnp.int32)[:, None]
    colsq = jnp.arange(width, dtype=jnp.int32)[None, :]
    index = (rowsp - colsq) % width
    table = taps.astype(jnp.float32).T[:, index]
    lower = rowsp >= colsq
    zero = jnp.zeros_like(table)
    return jnp.where(lower[None], table, zero), jnp.where(lower[None], zero, table)


def to_blocks(source, width):
    channels = source.shape[1]
    return source.astype(jnp.float32).reshape(-1, width, channels)


def causal_long(source, taps):
    width = taps.shape[0]
    blocks = to_blocks(source, width)
    before = jnp.concatenate([jnp.zeros_like(blocks[:1]), blocks[:-1]], 0)
    lower, upper = toeplitz_parts(taps)
    hi = lax.Precision.HIGHEST
    out = jnp.einsum('cpq,bqc->bpc', lower, blocks, precision=hi)
    out = out + jnp.einsum('cpq,bqc->bpc', upper, before, precision=hi)
    return out.reshape(source.shape)


def anti_long(source, taps):
    width = taps.shape[0]
    blocks = to_blocks(source, width)
    after = jnp.concatenate([blocks[1:], jnp.zeros_like(blocks[:1])], 0)
    lower, upper = toeplitz_parts(taps)
    hi = lax.Precision.HIGHEST
    out = jnp.einsum('cqp,bqc->bpc', lower, blocks, precision=hi)
    out = out + jnp.einsum('cqp,bqc->bpc', upper, after, precision=hi)
    return out.reshape(source.shape)


def filter_long(grad, source, width):
    blocks = to_blocks(source, width)
    before = jnp.concatenate([jnp.zeros_like(blocks[:1]), blocks[:-1]], 0)
    window = jnp.concatenate([before, blocks], 1)
    gradb = to_blocks(grad, width)
    moments = jnp.einsum('bpc,brc->cpr', gradb, window, precision=lax.Precision.HIGHEST)
    rowsp = jnp.arange(width, dtype=jnp.int32)[:, None]
    lagj = jnp.arange(width, dtype=jnp.int32)[None, :]
    index = (width + rowsp - lagj).astype(jnp.int32)
    picked = jnp.take_along_axis(moments, index[None], axis=2)
    return jnp.sum(picked, axis=1).T


def one_block(pieces):
    key_gate, values, query_gate, grad_output, short_taps, long_taps = pieces
    product = (key_gate.astype(jnp.float32) * values.astype(jnp.float32)).astype(jnp.bfloat16)
    short_out = causal_short(product, short_taps).astype(jnp.bfloat16)
    mixed = causal_long(short_out, long_taps)
    grad_query = (grad_output.astype(jnp.float32) * mixed).astype(jnp.bfloat16)
    grad_mixed = (grad_output.astype(jnp.float32) * query_gate.astype(jnp.float32)).astype(jnp.bfloat16)
    grad_short_out = anti_long(grad_mixed, long_taps).astype(jnp.bfloat16)
    grad_product = anti_short(grad_short_out, short_taps)
    grad_key = (grad_product * values.astype(jnp.float32)).astype(jnp.bfloat16)
    grad_value = (grad_product * key_gate.astype(jnp.float32)).astype(jnp.bfloat16)
    grad_long = filter_long(grad_mixed, short_out, long_taps.shape[0])
    grad_short = filter_short(grad_short_out, product, short_taps.shape[0])
    return grad_query, grad_key, grad_value, grad_long, grad_short


def split_channels(source, block):
    rows = source.shape[0]
    return source.reshape(rows, -1, block).transpose(1, 0, 2)


def join_channels(source):
    return source.transpose(1, 0, 2).reshape(source.shape[1], -1)


def reference(key_gate, values, query_gate, grad_output, short_taps, long_taps):
    block = math.gcd(D, 512)
    pieces = tuple(split_channels(item, block) for item in (key_gate, values, query_gate, grad_output, short_taps, long_taps))
    results = lax.map(one_block, pieces)
    grad_query = join_channels(results[0])
    grad_key = join_channels(results[1])
    grad_value = join_channels(results[2])
    grad_long = join_channels(results[3])
    grad_short = join_channels(results[4])
    return (grad_query, grad_key, grad_value, grad_long, grad_short)
```

```python
import functools

import jax
import jax.numpy as jnp
from jax import lax
from jax.experimental import pallas as pl
from jax.experimental.pallas import tpu as pltpu
from jax.sharding import PartitionSpec as P

MESH = pl.DeviceIdType.MESH
NX, NZ = 4, 16


def passed_along(shard, axis, by):
    length = lax.axis_size(axis)
    pairs = [(i, i + by) for i in range(length) if 0 <= i + by < length]
    return lax.ppermute(shard, axis, pairs)


def depthwise(extended, kernel):
    channels = kernel.shape[2]
    result = lax.conv_general_dilated(
        extended[None],
        kernel,
        (1,),
        [(0, 0)],
        dimension_numbers=("NWC", "WIO", "NWC"),
        feature_group_count=channels,
        preferred_element_type=jnp.float32,
    )
    return result[0]


def causal_apply(extended, weights):
    return depthwise(extended, jnp.flip(weights, 0)[:, None, :])


def forward_apply(extended, weights):
    return depthwise(extended, weights[:, None, :])


def filter_partial(history, grad):
    return jnp.flip(depthwise(history, grad[:, None, :]), 0)


def reduce_kernel(
    long_ref, short_ref, long_out, short_out,
    send_a, recv_a, send_s, recv_s, acc, send_z, recv_z, gath,
    sem_sa, sem_ra, sem_ss, sem_rs, sem_sz, sem_rz, sem_sg, sem_rg,
):
    seq = lax.axis_index("seq")
    chan = lax.axis_index("chan")
    x = seq // NZ
    z = seq % NZ

    def at_x(d):
        return ((x + d) % NX) * NZ + z

    def at_z(d):
        return x * NZ + (z + d) % NZ

    barrier = pltpu.get_barrier_semaphore()
    for d in range(1, NX):
        pl.semaphore_signal(barrier, inc=1, device_id=(at_x(d), chan), device_id_type=MESH)
    for d in range(1, NZ):
        pl.semaphore_signal(barrier, inc=1, device_id=(at_z(d), chan), device_id_type=MESH)
    for k in range(NX):
        send_a[k] = long_ref[32 * k : 32 * k + 32, :].astype(jnp.bfloat16)
        send_s[k] = short_ref[:, 256 * k : 256 * k + 256]
    pl.semaphore_wait(barrier, NX + NZ - 2)

    copies = []
    for d in range(1, NX):
        to = (x + d) % NX
        for src, dst, ss, rs in ((send_a, recv_a, sem_sa, sem_ra), (send_s, recv_s, sem_ss, sem_rs)):
            copy = pltpu.make_async_remote_copy(
                src_ref=src.at[to], dst_ref=dst.at[d - 1],
                send_sem=ss.at[d - 1], recv_sem=rs.at[d - 1],
                device_id=(at_x(d), chan), device_id_type=MESH,
            )
            copy.start()
            copies.append(copy)
    total = long_ref[pl.ds(pl.multiple_of(x * 32, 32), 32), :]
    stotal = send_s[x]
    for copy in copies:
        copy.wait()
    for d in range(1, NX):
        total = total + recv_a[d - 1].astype(jnp.float32)
        stotal = stotal + recv_s[d - 1]
    acc[...] = total
    tail = jnp.concatenate(
        [
            jnp.concatenate([stotal[r : r + 1] for r in range(4 * h, 4 * h + 4)], axis=1)
            for h in range(2)
        ],
        axis=0,
    )
    for k in range(NZ):
        send_z[k] = jnp.concatenate([acc[2 * k : 2 * k + 2, :], tail], axis=0).astype(jnp.bfloat16)
    copies = []
    for d in range(1, NZ):
        copy = pltpu.make_async_remote_copy(
            src_ref=send_z.at[(z + d) % NZ], dst_ref=recv_z.at[z],
            send_sem=sem_sz.at[d - 1], recv_sem=sem_rz.at[d - 1],
            device_id=(at_z(d), chan), device_id_type=MESH,
        )
        copy.start()
        copies.append(copy)
    recv_z[z] = send_z[z]
    for copy in copies:
        copy.wait()
    both = recv_z[0].astype(jnp.float32)
    for k in range(1, NZ):
        both = both + recv_z[k].astype(jnp.float32)
    long_out[...] = both[0:2]
    mine = jnp.concatenate(
        [both[2 + r // 4 : 3 + r // 4, 256 * (r % 4) : 256 * (r % 4) + 256] for r in range(8)], axis=0
    )
    gath[x] = mine
    copies = []
    for d in range(1, NX):
        copy = pltpu.make_async_remote_copy(
            src_ref=gath.at[x], dst_ref=gath.at[x],
            send_sem=sem_sg.at[d - 1], recv_sem=sem_rg.at[d - 1],
            device_id=(at_x(d), chan), device_id_type=MESH,
        )
        copy.start()
        copies.append(copy)
    for copy in copies:
        copy.wait()
    for k in range(NX):
        short_out[:, 256 * k : 256 * k + 256] = gath[k]


def reduce_both(long_part, short_part):
    chans = long_part.shape[1]
    vmem = pl.BlockSpec(memory_space=pltpu.VMEM)
    dma = pltpu.SemaphoreType.DMA
    return pl.pallas_call(
        reduce_kernel,
        out_shape=(
            jax.ShapeDtypeStruct((2, chans), jnp.float32),
            jax.ShapeDtypeStruct((8, chans), jnp.float32),
        ),
        in_specs=[vmem, vmem],
        out_specs=(vmem, vmem),
        scratch_shapes=[
            pltpu.VMEM((NX, 32, chans), jnp.bfloat16),
            pltpu.VMEM((NX - 1, 32, chans), jnp.bfloat16),
            pltpu.VMEM((NX, 8, chans // NX), jnp.float32),
            pltpu.VMEM((NX - 1, 8, chans // NX), jnp.float32),
            pltpu.VMEM((32, chans), jnp.float32),
            pltpu.VMEM((NZ, 4, chans), jnp.bfloat16),
            pltpu.VMEM((NZ, 4, chans), jnp.bfloat16),
            pltpu.VMEM((NX, 8, chans // NX), jnp.float32),
            dma((NX - 1,)), dma((NX - 1,)), dma((NX - 1,)), dma((NX - 1,)),
            dma((NZ - 1,)), dma((NZ - 1,)), dma((NX - 1,)), dma((NX - 1,)),
        ],
        compiler_params=pltpu.CompilerParams(collective_id=1, has_side_effects=True),
        name="reduce_both",
    )(long_part, short_part)


def body(key_gate, values, query_gate, grad_output, short_taps, long_taps):
    long_len = long_taps.shape[0]
    short_len = short_taps.shape[0]
    halo = long_len + short_len - 2
    row_count = key_gate.shape[0]
    product = (key_gate.astype(jnp.float32) * values.astype(jnp.float32)).astype(jnp.bfloat16)
    before = passed_along(product[row_count - halo :], "seq", 1)
    cotangent = lax.all_to_all(grad_output, "chan", split_axis=1, concat_axis=0, tiled=True)
    grad_mixed = (cotangent.astype(jnp.float32) * query_gate.astype(jnp.float32)).astype(
        jnp.bfloat16
    )
    after = passed_along(grad_mixed[:halo], "seq", -1)
    product_ext = jnp.concatenate([before, product], 0)
    long_ext = causal_apply(product_ext, short_taps).astype(jnp.bfloat16)
    mixed = causal_apply(long_ext, long_taps)
    grad_query = (cotangent.astype(jnp.float32) * mixed).astype(jnp.bfloat16)
    long_back = jnp.concatenate([grad_mixed, after], 0)
    short_back = forward_apply(long_back, long_taps).astype(jnp.bfloat16)
    grad_product = forward_apply(short_back, short_taps)
    grad_key = (grad_product * values.astype(jnp.float32)).astype(jnp.bfloat16)
    grad_value = (grad_product * key_gate.astype(jnp.float32)).astype(jnp.bfloat16)
    long_part = filter_partial(long_ext, grad_mixed)
    short_part = filter_partial(product_ext[long_len - 1 :], short_back[:row_count])
    short_part = jnp.pad(short_part, ((0, 1), (0, 0)))
    grad_long, grad_short = reduce_both(long_part, short_part)
    return (grad_query, grad_key, grad_value, grad_long, grad_short[:short_len])


def solution(mesh):
    in_specs = (
        P("seq", "chan"),
        P("seq", "chan"),
        P("seq", "chan"),
        P(("seq", "chan"), None),
        P(None, "chan"),
        P(None, "chan"),
    )
    out_specs = (
        P("seq", "chan"),
        P("seq", "chan"),
        P("seq", "chan"),
        P("seq", "chan"),
        P(None, "chan"),
    )
    return jax.shard_map(body, mesh=mesh, in_specs=in_specs, out_specs=out_specs, check_vma=False)
```

```python
import jax
import jax.numpy as jnp
from jax import lax
from jax.experimental import pallas as pl
from jax.experimental.pallas import tpu as pltpu
from jax.sharding import PartitionSpec as P

MESH = pl.DeviceIdType.MESH
NX, NZ, NC = 4, 16, 8
NSEQ = NX * NZ
HALO = 144
LANES = 128

F32 = jnp.float32
BF16 = jnp.bfloat16


def remote(src, dst, send, recv, device):
    return pltpu.make_async_remote_copy(
        src_ref=src, dst_ref=dst, send_sem=send, recv_sem=recv,
        device_id=device, device_id_type=MESH,
    )


def kernel(
    key_ref, val_ref, query_ref, go_ref, st_ref, lt_ref,
    gq_ref, gk_ref, gv_ref, long_out, short_out,
    cot, send_p, halo_p, send_g, halo_g, ext, gext, soext, shifted, gshift, mixed, gs,
    lp, send_a, recv_a, send_z, recv_z, sp, send_s, recv_s, send_t, recv_t, gath,
    sem_own, sem_c, rem_c, sem_p, rem_p, sem_g, rem_g, sem_a, rem_a, sem_z, rem_z,
    sem_s, rem_s, sem_t, rem_t, sem_h, rem_h,
):
    rows, chans = key_ref.shape
    groups = chans // LANES
    short_len = st_ref.shape[0]
    seq = lax.axis_index("seq")
    chan = lax.axis_index("chan")
    x = seq // NZ
    z = seq % NZ
    following = (seq + 1) % NSEQ
    preceding = (seq + NSEQ - 1) % NSEQ

    def at_x(d):
        return ((x + d) % NX) * NZ + z

    def at_z(d):
        return x * NZ + (z + d) % NZ

    def lanes(c):
        return pl.ds(pl.multiple_of(c * LANES, LANES), LANES)

    barrier = pltpu.get_barrier_semaphore()
    peers = [(seq, (chan + d) % NC) for d in range(1, NC)]
    peers += [(following, chan), (preceding, chan)]
    peers += [(at_x(d), chan) for d in range(1, NX)] + [(at_z(d), chan) for d in range(1, NZ)]
    for peer in peers:
        pl.semaphore_signal(barrier, inc=1, device_id=peer, device_id_type=MESH)

    def gate(c, carry):
        product = (key_ref[:, lanes(c)].astype(F32) * val_ref[:, lanes(c)].astype(F32)).astype(BF16)
        send_p[:, lanes(c)] = product[rows - HALO :]
        ext[c, HALO:, :] = product.astype(F32)
        return carry

    lax.fori_loop(0, groups, gate, 0)
    pl.semaphore_wait(barrier, len(peers))

    own = pltpu.make_async_copy(
        go_ref.at[:, pl.ds(pl.multiple_of(chan * chans, chans), chans)], cot.at[chan], sem_own
    )
    own.start()
    tokens = []
    for d in range(1, NC):
        to = (chan + d) % NC
        tokens.append(
            remote(
                go_ref.at[:, pl.ds(pl.multiple_of(to * chans, chans), chans)], cot.at[chan],
                sem_c.at[d - 1], rem_c.at[d - 1], (seq, to),
            )
        )
    for copy in tokens:
        copy.start()
    ahead = remote(send_p, halo_p, sem_p, rem_p, (following, chan))
    ahead.start()

    def short_rows(c, low, high):
        total = jnp.zeros((high - low, LANES), F32)
        for i in range(short_len):
            tap = st_ref[i : i + 1, lanes(c)].astype(F32)
            total = total + tap * ext[c, low + 16 - i : high + 16 - i, :]
        return total.astype(BF16).astype(F32)

    def long_tile(c, table, start, size, sign):
        def taps(q, acc):
            eight = lt_ref[pl.ds(pl.multiple_of(q * 8, 8), 8), lanes(c)]
            at = pl.multiple_of(start + sign * q * 8, 8)
            for s in range(8):
                acc = acc + eight[s : s + 1] * table[c, s, pl.ds(at, size), :]
            return acc

        return lax.fori_loop(0, 16, taps, jnp.zeros((size, LANES), F32))

    def later(c, carry):
        soext[136:384, :] = short_rows(c, 136, 384)
        for s in range(8):
            shifted[c, s, 144:384, :] = soext[144 - s : 384 - s, :]
        mixed[136:256, lanes(c)] = long_tile(c, shifted, 264, 120, -1)
        return carry

    lax.fori_loop(0, groups, later, 0)
    ahead.wait()

    def earlier(c, carry):
        ext[c, :HALO, :] = jnp.where(seq > 0, halo_p[:, lanes(c)].astype(F32), 0.0)
        soext[0:144, :] = short_rows(c, 0, 144)
        for s in range(8):
            shifted[c, s, 8:144, :] = soext[8 - s : 144 - s, :]
        mixed[0:136, lanes(c)] = long_tile(c, shifted, 128, 136, -1)
        return carry

    lax.fori_loop(0, groups, earlier, 0)
    own.wait()
    for copy in tokens:
        copy.wait()

    def outer(c, carry):
        got = cot[:, :, lanes(c)].reshape(rows, LANES).astype(F32)
        product = (got * query_ref[:, lanes(c)].astype(F32)).astype(BF16)
        send_g[:, lanes(c)] = product[:HALO]
        gext[c, :rows, :] = product.astype(F32)
        gq_ref[:, lanes(c)] = (got * mixed[:, lanes(c)]).astype(BF16)
        return carry

    lax.fori_loop(0, groups, outer, 0)
    back = remote(send_g, halo_g, sem_g, rem_g, (preceding, chan))
    back.start()

    def correlate(c, carry):
        def lags(q, inner):
            sums = [jnp.zeros((8, LANES), F32) for _ in range(8)]
            for part in range(4):
                grads = gext[c, 64 * part : 64 * part + 64, :]
                at = pl.multiple_of(128 + 64 * part - q * 8, 8)
                for s in range(8):
                    terms = grads * shifted[c, s, pl.ds(at, 64), :]
                    sums[s] = sums[s] + jnp.sum(terms.reshape(8, 8, LANES), axis=0)
            lp[pl.ds(pl.multiple_of(q * 8, 8), 8), lanes(c)] = jnp.concatenate(
                [jnp.sum(item, axis=0, keepdims=True) for item in sums], axis=0
            )
            return inner

        return lax.fori_loop(0, 16, lags, carry)

    lax.fori_loop(0, groups, correlate, 0)
    for k in range(NX):
        send_a[k] = lp[32 * k : 32 * k + 32, :].astype(BF16)
    back.wait()

    def backward(c, carry):
        gext[c, rows:, :] = jnp.where(seq < NSEQ - 1, halo_g[:, lanes(c)].astype(F32), 0.0)
        for s in range(8):
            gshift[c, s, :, :] = gext[c, s : s + 384, :]
        gs[0:128, :] = long_tile(c, gshift, 0, 128, 1).astype(BF16).astype(F32)
        gs[128:264, :] = long_tile(c, gshift, 128, 136, 1).astype(BF16).astype(F32)
        total = jnp.zeros((rows, LANES), F32)
        sums = []
        here = gs[0:rows, :]
        for i in range(short_len):
            tap = st_ref[i : i + 1, lanes(c)].astype(F32)
            total = total + tap * gs[i : i + rows, :]
            sums.append(jnp.sum(here * ext[c, HALO - i : HALO - i + rows, :], axis=0, keepdims=True))
        sums.append(jnp.zeros((1, LANES), F32))
        sp[:, lanes(c)] = jnp.concatenate(sums, axis=0)
        gk_ref[:, lanes(c)] = (total * val_ref[:, lanes(c)].astype(F32)).astype(BF16)
        gv_ref[:, lanes(c)] = (total * key_ref[:, lanes(c)].astype(F32)).astype(BF16)
        return carry

    first = [
        remote(send_a.at[(x + d) % NX], recv_a.at[d - 1], sem_a.at[d - 1], rem_a.at[d - 1], (at_x(d), chan))
        for d in range(1, NX)
    ]
    for copy in first:
        copy.start()
    lax.fori_loop(0, groups // 2, backward, 0)
    for copy in first:
        copy.wait()
    summed = lp[pl.ds(pl.multiple_of(x * 32, 32), 32), :]
    for d in range(1, NX):
        summed = summed + recv_a[d - 1].astype(F32)
    lp[0:32, :] = summed
    for k in range(NZ):
        send_z[k] = lp[2 * k : 2 * k + 2, :].astype(BF16)
    second = [
        remote(send_z.at[(z + d) % NZ], recv_z.at[d - 1], sem_z.at[d - 1], rem_z.at[d - 1], (at_z(d), chan))
        for d in range(1, NZ)
    ]
    for copy in second:
        copy.start()
    lax.fori_loop(groups // 2, groups, backward, 0)

    width = chans // NX
    for k in range(NX):
        send_s[k] = sp[:, width * k : width * k + width]
    third = [
        remote(send_s.at[(x + d) % NX], recv_s.at[d - 1], sem_s.at[d - 1], rem_s.at[d - 1], (at_x(d), chan))
        for d in range(1, NX)
    ]
    for copy in third:
        copy.start()
    for copy in second:
        copy.wait()
    both = send_z[z].astype(F32)
    for d in range(1, NZ):
        both = both + recv_z[d - 1].astype(F32)
    long_out[...] = both
    for copy in third:
        copy.wait()
    mine = send_s[x]
    for d in range(1, NX):
        mine = mine + recv_s[d - 1]
    send_t[...] = mine.astype(BF16)
    fourth = [
        remote(send_t, recv_t.at[z], sem_t.at[d - 1], rem_t.at[d - 1], (at_z(d), chan))
        for d in range(1, NZ)
    ]
    for copy in fourth:
        copy.start()
    recv_t[z] = mine.astype(BF16)
    for copy in fourth:
        copy.wait()
    mine = recv_t[0].astype(F32)
    for k in range(1, NZ):
        mine = mine + recv_t[k].astype(F32)
    gath[x] = mine
    fifth = [
        remote(gath.at[x], gath.at[x], sem_h.at[d - 1], rem_h.at[d - 1], (at_x(d), chan))
        for d in range(1, NX)
    ]
    for copy in fifth:
        copy.start()
    for copy in fifth:
        copy.wait()
    for k in range(NX):
        short_out[:, width * k : width * k + width] = gath[k]


def body(key_gate, values, query_gate, grad_output, short_taps, long_taps):
    rows, chans = key_gate.shape
    groups = chans // LANES
    width = chans // NX
    vmem = pl.BlockSpec(memory_space=pltpu.VMEM)
    dma = pltpu.SemaphoreType.DMA
    V = pltpu.VMEM
    grad_query, grad_key, grad_value, grad_long, grad_short = pl.pallas_call(
        kernel,
        out_shape=(
            jax.ShapeDtypeStruct((rows, chans), BF16),
            jax.ShapeDtypeStruct((rows, chans), BF16),
            jax.ShapeDtypeStruct((rows, chans), BF16),
            jax.ShapeDtypeStruct((2, chans), F32),
            jax.ShapeDtypeStruct((8, chans), F32),
        ),
        in_specs=[vmem, vmem, vmem, pl.BlockSpec(memory_space=pl.ANY), vmem, vmem],
        out_specs=(vmem,) * 5,
        scratch_shapes=[
            V((NC, rows // NC, chans), BF16),
            V((HALO, chans), BF16), V((HALO, chans), BF16),
            V((HALO, chans), BF16), V((HALO, chans), BF16),
            V((groups, HALO + rows, LANES), F32), V((groups, HALO + rows, LANES), F32),
            V((384, LANES), F32),
            V((groups, 8, 384, LANES), F32), V((groups, 8, 384, LANES), F32),
            V((rows, chans), F32), V((264, LANES), F32),
            V((128, chans), F32),
            V((NX, 32, chans), BF16), V((NX - 1, 32, chans), BF16),
            V((NZ, 2, chans), BF16), V((NZ - 1, 2, chans), BF16),
            V((8, chans), F32), V((NX, 8, width), F32), V((NX - 1, 8, width), F32),
            V((8, width), BF16), V((NZ, 8, width), BF16), V((NX, 8, width), F32),
            dma, dma((NC - 1,)), dma((NC - 1,)), dma, dma, dma, dma,
            dma((NX - 1,)), dma((NX - 1,)), dma((NZ - 1,)), dma((NZ - 1,)),
            dma((NX - 1,)), dma((NX - 1,)), dma((NZ - 1,)), dma((NZ - 1,)),
            dma((NX - 1,)), dma((NX - 1,)),
        ],
        compiler_params=pltpu.CompilerParams(
            collective_id=1, has_side_effects=True, vmem_limit_bytes=60 * 1024 * 1024
        ),
        name="conv_chain",
    )(key_gate, values, query_gate, grad_output, short_taps, long_taps.astype(F32))
    return (grad_query, grad_key, grad_value, grad_long, grad_short[: short_taps.shape[0]])


def solution(mesh):
    in_specs = (
        P("seq", "chan"),
        P("seq", "chan"),
        P("seq", "chan"),
        P(("seq", "chan"), None),
        P(None, "chan"),
        P(None, "chan"),
    )
    out_specs = (
        P("seq", "chan"),
        P("seq", "chan"),
        P("seq", "chan"),
        P("seq", "chan"),
        P(None, "chan"),
    )
    return jax.shard_map(body, mesh=mesh, in_specs=in_specs, out_specs=out_specs, check_vma=False)
```

```python
import jax
import jax.numpy as jnp
from jax import lax
from jax.experimental import pallas as pl
from jax.experimental.pallas import tpu as pltpu
from jax.sharding import PartitionSpec as P

MESH = pl.DeviceIdType.MESH
NX, NZ, NC = 4, 16, 8
NSEQ = NX * NZ
HALO = 144
LANES = 128

F32 = jnp.float32
BF16 = jnp.bfloat16


def remote(src, dst, send, recv, device):
    return pltpu.make_async_remote_copy(
        src_ref=src, dst_ref=dst, send_sem=send, recv_sem=recv,
        device_id=device, device_id_type=MESH,
    )


def kernel(
    key_ref, val_ref, query_ref, go_ref, st_ref, lt_ref,
    gq_ref, gk_ref, gv_ref, long_out, short_out,
    ltf, cot, send_p, halo_p, send_g, halo_g, ext, gext, soext, shifted, gshift, mixed, gs,
    lp, send_a, recv_a, send_z, recv_z, sp, send_s, recv_s, send_t, recv_t, gath,
    sem_own, sem_c, rem_c, sem_p, rem_p, sem_g, rem_g, sem_a, rem_a, sem_z, rem_z,
    sem_s, rem_s, sem_t, rem_t, sem_h, rem_h,
):
    rows, chans = key_ref.shape
    groups = chans // LANES
    short_len = st_ref.shape[0]
    seq = lax.axis_index("seq")
    chan = lax.axis_index("chan")
    x = seq // NZ
    z = seq % NZ
    following = (seq + 1) % NSEQ
    preceding = (seq + NSEQ - 1) % NSEQ

    def at_x(d):
        return ((x + d) % NX) * NZ + z

    def at_z(d):
        return x * NZ + (z + d) % NZ

    def lanes(c):
        return pl.ds(pl.multiple_of(c * LANES, LANES), LANES)

    barrier = pltpu.get_barrier_semaphore()
    peers = [(seq, (chan + d) % NC) for d in range(1, NC)]
    peers += [(following, chan), (preceding, chan)]
    peers += [(at_x(d), chan) for d in range(1, NX)] + [(at_z(d), chan) for d in range(1, NZ)]
    for peer in peers:
        pl.semaphore_signal(barrier, inc=1, device_id=peer, device_id_type=MESH)

    ltf[...] = lt_ref[...].astype(F32)

    def gate(c, carry):
        product = (key_ref[:, lanes(c)].astype(F32) * val_ref[:, lanes(c)].astype(F32)).astype(BF16)
        send_p[:, lanes(c)] = product[rows - HALO :]
        ext[c, HALO:, :] = product.astype(F32)
        return carry

    lax.fori_loop(0, groups, gate, 0)
    pl.semaphore_wait(barrier, len(peers))

    own = pltpu.make_async_copy(
        go_ref.at[:, pl.ds(pl.multiple_of(chan * chans, chans), chans)], cot.at[chan], sem_own
    )
    own.start()
    tokens = []
    for d in range(1, NC):
        to = (chan + d) % NC
        tokens.append(
            remote(
                go_ref.at[:, pl.ds(pl.multiple_of(to * chans, chans), chans)], cot.at[chan],
                sem_c.at[d - 1], rem_c.at[d - 1], (seq, to),
            )
        )
    for copy in tokens:
        copy.start()
    ahead = remote(send_p, halo_p, sem_p, rem_p, (following, chan))
    ahead.start()

    def short_rows(c, low, high):
        total = jnp.zeros((high - low, LANES), F32)
        for i in range(short_len):
            tap = st_ref[i : i + 1, lanes(c)].astype(F32)
            total = total + tap * ext[c, low + 16 - i : high + 16 - i, :]
        return total.astype(BF16).astype(F32)

    def long_tile(c, table, start, size, sign):
        def taps(q, acc):
            eight = ltf[pl.ds(pl.multiple_of(q * 8, 8), 8), lanes(c)]
            at = pl.multiple_of(start + sign * q * 8, 8)
            for s in range(8):
                acc = acc + eight[s : s + 1] * table[c, s, pl.ds(at, size), :]
            return acc

        return lax.fori_loop(0, 16, taps, jnp.zeros((size, LANES), F32))

    def later(c, carry):
        soext[136:384, :] = short_rows(c, 136, 384)
        for s in range(8):
            shifted[c, s, 144:384, :] = soext[144 - s : 384 - s, :]
        mixed[136:256, lanes(c)] = long_tile(c, shifted, 264, 120, -1)
        return carry

    lax.fori_loop(0, groups, later, 0)
    ahead.wait()

    def history(c, carry):
        ext[c, :HALO, :] = jnp.where(seq > 0, halo_p[:, lanes(c)].astype(F32), 0.0)
        soext[0:144, :] = short_rows(c, 0, 144)
        for s in range(8):
            shifted[c, s, 8:144, :] = soext[8 - s : 144 - s, :]
        return carry

    lax.fori_loop(0, groups, history, 0)
    own.wait()
    for copy in tokens:
        copy.wait()

    def outer(c, carry):
        got = cot[:, :, lanes(c)].reshape(rows, LANES).astype(F32)
        product = (got * query_ref[:, lanes(c)].astype(F32)).astype(BF16)
        send_g[:, lanes(c)] = product[:HALO]
        gext[c, :rows, :] = product.astype(F32)
        return carry

    lax.fori_loop(0, groups, outer, 0)
    back = remote(send_g, halo_g, sem_g, rem_g, (preceding, chan))
    back.start()

    def correlate(c, carry):
        def lags(q, inner):
            sums = [jnp.zeros((8, LANES), F32) for _ in range(8)]
            for part in range(4):
                grads = gext[c, 64 * part : 64 * part + 64, :]
                at = pl.multiple_of(128 + 64 * part - q * 8, 8)
                for s in range(8):
                    terms = grads * shifted[c, s, pl.ds(at, 64), :]
                    sums[s] = sums[s] + jnp.sum(terms.reshape(8, 8, LANES), axis=0)
            lp[pl.ds(pl.multiple_of(q * 8, 8), 8), lanes(c)] = jnp.concatenate(
                [jnp.sum(item, axis=0, keepdims=True) for item in sums], axis=0
            )
            return inner

        return lax.fori_loop(0, 16, lags, carry)

    lax.fori_loop(0, groups, correlate, 0)
    for k in range(NX):
        send_a[k] = lp[32 * k : 32 * k + 32, :].astype(BF16)
    back.wait()

    def backward(c, carry):
        gext[c, rows:, :] = jnp.where(seq < NSEQ - 1, halo_g[:, lanes(c)].astype(F32), 0.0)
        for s in range(8):
            gshift[c, s, :, :] = gext[c, s : s + 384, :]
        gs[0:128, :] = long_tile(c, gshift, 0, 128, 1).astype(BF16).astype(F32)
        gs[128:264, :] = long_tile(c, gshift, 128, 136, 1).astype(BF16).astype(F32)
        total = jnp.zeros((rows, LANES), F32)
        sums = []
        here = gs[0:rows, :]
        for i in range(short_len):
            tap = st_ref[i : i + 1, lanes(c)].astype(F32)
            total = total + tap * gs[i : i + rows, :]
            sums.append(jnp.sum(here * ext[c, HALO - i : HALO - i + rows, :], axis=0, keepdims=True))
        sums.append(jnp.zeros((1, LANES), F32))
        sp[:, lanes(c)] = jnp.concatenate(sums, axis=0)
        gk_ref[:, lanes(c)] = (total * val_ref[:, lanes(c)].astype(F32)).astype(BF16)
        gv_ref[:, lanes(c)] = (total * key_ref[:, lanes(c)].astype(F32)).astype(BF16)
        return carry

    first = [
        remote(send_a.at[(x + d) % NX], recv_a.at[d - 1], sem_a.at[d - 1], rem_a.at[d - 1], (at_x(d), chan))
        for d in range(1, NX)
    ]
    for copy in first:
        copy.start()
    lax.fori_loop(0, groups // 2, backward, 0)
    for copy in first:
        copy.wait()
    summed = lp[pl.ds(pl.multiple_of(x * 32, 32), 32), :]
    for d in range(1, NX):
        summed = summed + recv_a[d - 1].astype(F32)
    lp[0:32, :] = summed
    for k in range(NZ):
        send_z[k] = lp[2 * k : 2 * k + 2, :].astype(BF16)
    second = [
        remote(send_z.at[(z + d) % NZ], recv_z.at[d - 1], sem_z.at[d - 1], rem_z.at[d - 1], (at_z(d), chan))
        for d in range(1, NZ)
    ]
    for copy in second:
        copy.start()
    lax.fori_loop(groups // 2, groups, backward, 0)

    def finish(c, carry):
        mixed[0:136, lanes(c)] = long_tile(c, shifted, 128, 136, -1)
        got = cot[:, :, lanes(c)].reshape(rows, LANES).astype(F32)
        gq_ref[:, lanes(c)] = (got * mixed[:, lanes(c)]).astype(BF16)
        return carry

    width = chans // NX
    for k in range(NX):
        send_s[k] = sp[:, width * k : width * k + width]
    third = [
        remote(send_s.at[(x + d) % NX], recv_s.at[d - 1], sem_s.at[d - 1], rem_s.at[d - 1], (at_x(d), chan))
        for d in range(1, NX)
    ]
    for copy in third:
        copy.start()
    for copy in second:
        copy.wait()
    both = send_z[z].astype(F32)
    for d in range(1, NZ):
        both = both + recv_z[d - 1].astype(F32)
    long_out[...] = both
    lax.fori_loop(0, 2, finish, 0)
    for copy in third:
        copy.wait()
    mine = send_s[x]
    for d in range(1, NX):
        mine = mine + recv_s[d - 1]
    send_t[...] = mine.astype(BF16)
    fourth = [
        remote(send_t, recv_t.at[z], sem_t.at[d - 1], rem_t.at[d - 1], (at_z(d), chan))
        for d in range(1, NZ)
    ]
    for copy in fourth:
        copy.start()
    recv_t[z] = mine.astype(BF16)
    lax.fori_loop(2, groups - 1, finish, 0)
    for copy in fourth:
        copy.wait()
    mine = recv_t[0].astype(F32)
    for k in range(1, NZ):
        mine = mine + recv_t[k].astype(F32)
    gath[x] = mine
    fifth = [
        remote(gath.at[x], gath.at[x], sem_h.at[d - 1], rem_h.at[d - 1], (at_x(d), chan))
        for d in range(1, NX)
    ]
    for copy in fifth:
        copy.start()
    lax.fori_loop(groups - 1, groups, finish, 0)
    for copy in fifth:
        copy.wait()
    for k in range(NX):
        short_out[:, width * k : width * k + width] = gath[k]


def body(key_gate, values, query_gate, grad_output, short_taps, long_taps):
    rows, chans = key_gate.shape
    groups = chans // LANES
    width = chans // NX
    vmem = pl.BlockSpec(memory_space=pltpu.VMEM)
    dma = pltpu.SemaphoreType.DMA
    V = pltpu.VMEM
    grad_query, grad_key, grad_value, grad_long, grad_short = pl.pallas_call(
        kernel,
        out_shape=(
            jax.ShapeDtypeStruct((rows, chans), BF16),
            jax.ShapeDtypeStruct((rows, chans), BF16),
            jax.ShapeDtypeStruct((rows, chans), BF16),
            jax.ShapeDtypeStruct((2, chans), F32),
            jax.ShapeDtypeStruct((8, chans), F32),
        ),
        in_specs=[vmem, vmem, vmem, pl.BlockSpec(memory_space=pl.ANY), vmem, vmem],
        out_specs=(vmem,) * 5,
        scratch_shapes=[
            V(long_taps.shape, F32),
            V((NC, rows // NC, chans), BF16),
            V((HALO, chans), BF16), V((HALO, chans), BF16),
            V((HALO, chans), BF16), V((HALO, chans), BF16),
            V((groups, HALO + rows, LANES), F32), V((groups, HALO + rows, LANES), F32),
            V((384, LANES), F32),
            V((groups, 8, 384, LANES), F32), V((groups, 8, 384, LANES), F32),
            V((rows, chans), F32), V((264, LANES), F32),
            V((128, chans), F32),
            V((NX, 32, chans), BF16), V((NX - 1, 32, chans), BF16),
            V((NZ, 2, chans), BF16), V((NZ - 1, 2, chans), BF16),
            V((8, chans), F32), V((NX, 8, width), F32), V((NX - 1, 8, width), F32),
            V((8, width), BF16), V((NZ, 8, width), BF16), V((NX, 8, width), F32),
            dma, dma((NC - 1,)), dma((NC - 1,)), dma, dma, dma, dma,
            dma((NX - 1,)), dma((NX - 1,)), dma((NZ - 1,)), dma((NZ - 1,)),
            dma((NX - 1,)), dma((NX - 1,)), dma((NZ - 1,)), dma((NZ - 1,)),
            dma((NX - 1,)), dma((NX - 1,)),
        ],
        compiler_params=pltpu.CompilerParams(
            collective_id=1, has_side_effects=True, vmem_limit_bytes=60 * 1024 * 1024
        ),
        name="conv_chain",
    )(key_gate, values, query_gate, grad_output, short_taps, long_taps)
    return (grad_query, grad_key, grad_value, grad_long, grad_short[: short_taps.shape[0]])


def solution(mesh):
    in_specs = (
        P("seq", "chan"),
        P("seq", "chan"),
        P("seq", "chan"),
        P(("seq", "chan"), None),
        P(None, "chan"),
        P(None, "chan"),
    )
    out_specs = (
        P("seq", "chan"),
        P("seq", "chan"),
        P("seq", "chan"),
        P("seq", "chan"),
        P(None, "chan"),
    )
    return jax.shard_map(body, mesh=mesh, in_specs=in_specs, out_specs=out_specs, check_vma=False)
```

```python
import jax
import jax.numpy as jnp
from jax import lax
from jax.experimental import pallas as pl
from jax.experimental.pallas import tpu as pltpu
from jax.sharding import PartitionSpec as P

MESH = pl.DeviceIdType.MESH
NX, NZ, NC = 4, 16, 8
NSEQ = NX * NZ
HALO = 144
LANES = 128

F32 = jnp.float32
BF16 = jnp.bfloat16


def tree(terms):
    while len(terms) > 1:
        terms = [terms[k] + terms[k + 1] for k in range(0, len(terms), 2)]
    return terms[0]


def remote(src, dst, send, recv, device):
    return pltpu.make_async_remote_copy(
        src_ref=src, dst_ref=dst, send_sem=send, recv_sem=recv,
        device_id=device, device_id_type=MESH,
    )


def kernel(
    key_ref, val_ref, query_ref, go_ref, st_ref, lt_ref,
    gq_ref, gk_ref, gv_ref, long_out, short_out,
    ltf, cot, send_p, halo_p, send_g, halo_g, ext, gext, soext, shifted, gshift, mixed, gs,
    lp, send_a, recv_a, send_z, recv_z, sp, send_s, recv_s, send_t, recv_t, gath,
    sem_own, sem_c, rem_c, sem_p, rem_p, sem_g, rem_g, sem_a, rem_a, sem_z, rem_z,
    sem_s, rem_s, sem_t, rem_t, sem_h, rem_h,
):
    rows, chans = key_ref.shape
    groups = chans // LANES
    short_len = st_ref.shape[0]
    seq = lax.axis_index("seq")
    chan = lax.axis_index("chan")
    x = seq // NZ
    z = seq % NZ
    following = (seq + 1) % NSEQ
    preceding = (seq + NSEQ - 1) % NSEQ

    def at_x(d):
        return ((x + d) % NX) * NZ + z

    def at_z(d):
        return x * NZ + (z + d) % NZ

    def lanes(c):
        return pl.ds(pl.multiple_of(c * LANES, LANES), LANES)

    barrier = pltpu.get_barrier_semaphore()
    peers = [(seq, (chan + d) % NC) for d in range(1, NC)]
    peers += [(following, chan), (preceding, chan)]
    peers += [(at_x(d), chan) for d in range(1, NX)] + [(at_z(d), chan) for d in range(1, NZ)]
    for peer in peers:
        pl.semaphore_signal(barrier, inc=1, device_id=peer, device_id_type=MESH)

    ltf[...] = lt_ref[...].astype(F32)

    def gate(c, carry):
        product = (key_ref[:, lanes(c)].astype(F32) * val_ref[:, lanes(c)].astype(F32)).astype(BF16)
        send_p[:, lanes(c)] = product[rows - HALO :]
        ext[c, HALO:, :] = product.astype(F32)
        return carry

    lax.fori_loop(0, groups, gate, 0)
    pl.semaphore_wait(barrier, len(peers))

    own = pltpu.make_async_copy(
        go_ref.at[:, pl.ds(pl.multiple_of(chan * chans, chans), chans)], cot.at[chan], sem_own
    )
    own.start()
    tokens = []
    for d in range(1, NC):
        to = (chan + d) % NC
        tokens.append(
            remote(
                go_ref.at[:, pl.ds(pl.multiple_of(to * chans, chans), chans)], cot.at[chan],
                sem_c.at[d - 1], rem_c.at[d - 1], (seq, to),
            )
        )
    for copy in tokens:
        copy.start()
    ahead = remote(send_p, halo_p, sem_p, rem_p, (following, chan))
    ahead.start()

    def short_rows(c, low, high):
        total = jnp.zeros((high - low, LANES), F32)
        for i in range(short_len):
            tap = st_ref[i : i + 1, lanes(c)].astype(F32)
            total = total + tap * ext[c, low + 16 - i : high + 16 - i, :]
        return total.astype(BF16).astype(F32)

    def long_tile(c, table, start, size, sign):
        def taps(q, acc):
            some = ltf[pl.ds(pl.multiple_of(q * 16, 16), 16), lanes(c)]
            at = start // 16 + sign * q
            terms = []
            for t in range(16):
                tap = jnp.broadcast_to(some[t : t + 1], (16, LANES)).astype(BF16)
                terms.append(tap[None] * table[c, t, pl.ds(at, size // 16)])
            return acc + tree(terms[:8]).astype(F32) + tree(terms[8:]).astype(F32)

        shape = (size // 16, 16, LANES)
        return lax.fori_loop(0, 8, taps, jnp.zeros(shape, F32)).reshape(size, LANES)

    def later(c, carry):
        soext[136:384, :] = short_rows(c, 136, 384)
        for s in range(16):
            shifted[c, s, 10:24] = soext[160 - s : 384 - s, :].astype(BF16).reshape(14, 16, LANES)
        mixed[144:256, lanes(c)] = long_tile(c, shifted, 272, 112, -1)
        return carry

    lax.fori_loop(0, groups, later, 0)
    ahead.wait()

    def history(c, carry):
        ext[c, :HALO, :] = jnp.where(seq > 0, halo_p[:, lanes(c)].astype(F32), 0.0)
        soext[0:160, :] = short_rows(c, 0, 160)
        for s in range(16):
            shifted[c, s, 1:10] = soext[16 - s : 160 - s, :].astype(BF16).reshape(9, 16, LANES)
        return carry

    lax.fori_loop(0, groups, history, 0)
    own.wait()
    for copy in tokens:
        copy.wait()

    def outer(c, carry):
        got = cot[:, :, lanes(c)].reshape(rows, LANES).astype(F32)
        product = (got * query_ref[:, lanes(c)].astype(F32)).astype(BF16)
        send_g[:, lanes(c)] = product[:HALO]
        gext[c, :rows, :] = product.astype(F32)
        return carry

    lax.fori_loop(0, groups, outer, 0)
    back = remote(send_g, halo_g, sem_g, rem_g, (preceding, chan))
    back.start()

    def correlate(c, carry):
        def lags(q, inner):
            sums = [jnp.zeros((16, LANES), F32) for _ in range(16)]
            for part in range(2):
                grads = gext[c, 128 * part : 128 * part + 128, :].astype(BF16).reshape(8, 16, LANES)
                for t in range(16):
                    terms = grads * shifted[c, t, pl.ds(8 + 8 * part - q, 8)]
                    sums[t] = sums[t] + tree([terms[k] for k in range(8)]).astype(F32)
            lp[pl.ds(pl.multiple_of(q * 16, 16), 16), lanes(c)] = jnp.concatenate(
                [jnp.sum(item, axis=0, keepdims=True) for item in sums], axis=0
            )
            return inner

        return lax.fori_loop(0, 8, lags, carry)

    lax.fori_loop(0, groups, correlate, 0)
    for k in range(NX):
        send_a[k] = lp[32 * k : 32 * k + 32, :].astype(BF16)
    back.wait()

    def backward(c, carry):
        gext[c, rows:, :] = jnp.where(seq < NSEQ - 1, halo_g[:, lanes(c)].astype(F32), 0.0)
        for s in range(16):
            gshift[c, s] = gext[c, s : s + 384, :].astype(BF16).reshape(24, 16, LANES)
        gs[0:128, :] = long_tile(c, gshift, 0, 128, 1).astype(BF16).astype(F32)
        gs[128:272, :] = long_tile(c, gshift, 128, 144, 1).astype(BF16).astype(F32)
        total = jnp.zeros((rows, LANES), F32)
        sums = []
        here = gs[0:rows, :]
        for i in range(short_len):
            tap = st_ref[i : i + 1, lanes(c)].astype(F32)
            total = total + tap * gs[i : i + rows, :]
            sums.append(jnp.sum(here * ext[c, HALO - i : HALO - i + rows, :], axis=0, keepdims=True))
        sums.append(jnp.zeros((1, LANES), F32))
        sp[:, lanes(c)] = jnp.concatenate(sums, axis=0)
        gk_ref[:, lanes(c)] = (total * val_ref[:, lanes(c)].astype(F32)).astype(BF16)
        gv_ref[:, lanes(c)] = (total * key_ref[:, lanes(c)].astype(F32)).astype(BF16)
        return carry

    first = [
        remote(send_a.at[(x + d) % NX], recv_a.at[d - 1], sem_a.at[d - 1], rem_a.at[d - 1], (at_x(d), chan))
        for d in range(1, NX)
    ]
    for copy in first:
        copy.start()
    lax.fori_loop(0, groups // 2, backward, 0)
    for copy in first:
        copy.wait()
    summed = lp[pl.ds(pl.multiple_of(x * 32, 32), 32), :]
    for d in range(1, NX):
        summed = summed + recv_a[d - 1].astype(F32)
    lp[0:32, :] = summed
    for k in range(NZ):
        send_z[k] = lp[2 * k : 2 * k + 2, :].astype(BF16)
    second = [
        remote(send_z.at[(z + d) % NZ], recv_z.at[d - 1], sem_z.at[d - 1], rem_z.at[d - 1], (at_z(d), chan))
        for d in range(1, NZ)
    ]
    for copy in second:
        copy.start()
    lax.fori_loop(groups // 2, groups, backward, 0)

    def finish(c, carry):
        mixed[0:144, lanes(c)] = long_tile(c, shifted, 128, 144, -1)
        got = cot[:, :, lanes(c)].reshape(rows, LANES).astype(F32)
        gq_ref[:, lanes(c)] = (got * mixed[:, lanes(c)]).astype(BF16)
        return carry

    width = chans // NX
    for k in range(NX):
        send_s[k] = sp[:, width * k : width * k + width]
    third = [
        remote(send_s.at[(x + d) % NX], recv_s.at[d - 1], sem_s.at[d - 1], rem_s.at[d - 1], (at_x(d), chan))
        for d in range(1, NX)
    ]
    for copy in third:
        copy.start()
    for copy in second:
        copy.wait()
    both = send_z[z].astype(F32)
    for d in range(1, NZ):
        both = both + recv_z[d - 1].astype(F32)
    long_out[...] = both
    lax.fori_loop(0, 2, finish, 0)
    for copy in third:
        copy.wait()
    mine = send_s[x]
    for d in range(1, NX):
        mine = mine + recv_s[d - 1]
    send_t[...] = mine.astype(BF16)
    fourth = [
        remote(send_t, recv_t.at[z], sem_t.at[d - 1], rem_t.at[d - 1], (at_z(d), chan))
        for d in range(1, NZ)
    ]
    for copy in fourth:
        copy.start()
    recv_t[z] = mine.astype(BF16)
    lax.fori_loop(2, groups - 1, finish, 0)
    for copy in fourth:
        copy.wait()
    mine = recv_t[0].astype(F32)
    for k in range(1, NZ):
        mine = mine + recv_t[k].astype(F32)
    gath[x] = mine
    fifth = [
        remote(gath.at[x], gath.at[x], sem_h.at[d - 1], rem_h.at[d - 1], (at_x(d), chan))
        for d in range(1, NX)
    ]
    for copy in fifth:
        copy.start()
    lax.fori_loop(groups - 1, groups, finish, 0)
    for copy in fifth:
        copy.wait()
    for k in range(NX):
        short_out[:, width * k : width * k + width] = gath[k]


def body(key_gate, values, query_gate, grad_output, short_taps, long_taps):
    rows, chans = key_gate.shape
    groups = chans // LANES
    width = chans // NX
    vmem = pl.BlockSpec(memory_space=pltpu.VMEM)
    dma = pltpu.SemaphoreType.DMA
    V = pltpu.VMEM
    grad_query, grad_key, grad_value, grad_long, grad_short = pl.pallas_call(
        kernel,
        out_shape=(
            jax.ShapeDtypeStruct((rows, chans), BF16),
            jax.ShapeDtypeStruct((rows, chans), BF16),
            jax.ShapeDtypeStruct((rows, chans), BF16),
            jax.ShapeDtypeStruct((2, chans), F32),
            jax.ShapeDtypeStruct((8, chans), F32),
        ),
        in_specs=[vmem, vmem, vmem, pl.BlockSpec(memory_space=pl.ANY), vmem, vmem],
        out_specs=(vmem,) * 5,
        scratch_shapes=[
            V(long_taps.shape, F32),
            V((NC, rows // NC, chans), BF16),
            V((HALO, chans), BF16), V((HALO, chans), BF16),
            V((HALO, chans), BF16), V((HALO, chans), BF16),
            V((groups, HALO + rows, LANES), F32), V((groups, HALO + rows, LANES), F32),
            V((384, LANES), F32),
            V((groups, 16, 24, 16, LANES), BF16), V((groups, 16, 24, 16, LANES), BF16),
            V((rows, chans), F32), V((272, LANES), F32),
            V((128, chans), F32),
            V((NX, 32, chans), BF16), V((NX - 1, 32, chans), BF16),
            V((NZ, 2, chans), BF16), V((NZ - 1, 2, chans), BF16),
            V((8, chans), F32), V((NX, 8, width), F32), V((NX - 1, 8, width), F32),
            V((8, width), BF16), V((NZ, 8, width), BF16), V((NX, 8, width), F32),
            dma, dma((NC - 1,)), dma((NC - 1,)), dma, dma, dma, dma,
            dma((NX - 1,)), dma((NX - 1,)), dma((NZ - 1,)), dma((NZ - 1,)),
            dma((NX - 1,)), dma((NX - 1,)), dma((NZ - 1,)), dma((NZ - 1,)),
            dma((NX - 1,)), dma((NX - 1,)),
        ],
        compiler_params=pltpu.CompilerParams(
            collective_id=1, has_side_effects=True, vmem_limit_bytes=60 * 1024 * 1024
        ),
        name="conv_chain",
    )(key_gate, values, query_gate, grad_output, short_taps, long_taps)
    return (grad_query, grad_key, grad_value, grad_long, grad_short[: short_taps.shape[0]])


def solution(mesh):
    in_specs = (
        P("seq", "chan"),
        P("seq", "chan"),
        P("seq", "chan"),
        P(("seq", "chan"), None),
        P(None, "chan"),
        P(None, "chan"),
    )
    out_specs = (
        P("seq", "chan"),
        P("seq", "chan"),
        P("seq", "chan"),
        P("seq", "chan"),
        P(None, "chan"),
    )
    return jax.shard_map(body, mesh=mesh, in_specs=in_specs, out_specs=out_specs, check_vma=False)
```
